1024 devices in a mesh: expert: 32 (over z, core), fsdp: 32 (over y, x).
Axes of the slice: x: 4, y: 8, z: 16, core: 2. Of those that a mesh axis runs over, the one named last changes fastest.
Arguments:
- tokens: bfloat16 [1024, 4096], P('expert', 'fsdp'), may hold values from -6 to 6
- expert_ids: int32 [1024, 8], P('expert'), may hold values from 0 to 63, all different within a row; in each aligned block of 32 rows (0 to 31, 32 to 63, ...) at most 8 rows name the same one
- gate_up: bfloat16 [64, 2, 1536, 4096], P('expert', None, 'fsdp'), may hold values from -0.09375 to 0.09375
- hidden_grad: bfloat16 [64, 1536, 256], P('expert', 'fsdp'), may hold values from -1.5 to 1.5
Outputs:
- hidden: bfloat16 [64, 1536, 256], P('expert', 'fsdp')
- gate_up_grad: bfloat16 [64, 2, 1536, 4096], P('expert', None, 'fsdp')
- tokens_grad: bfloat16 [1024, 4096], P('expert', 'fsdp')
The draws below stay inside these ranges and needn't reach their ends.
Inputs may be any that keep to these rules, and one draw needn't show every extreme that they name: `expert_ids`: each token names 8 different experts. Among the 32 tokens of each aligned block (the tokens of one expert index) no expert is named by more than 8 tokens, and in some block one expert is named by exactly 8.
All inputs are finite; a program needn't handle non-finite values.
Results may differ from the reference program's by a relative error of at most 0.017.
Values may be sent and summed in bfloat16 or wider, within the bound.
No kernel may reach another device: no remote copies, remote signals or barrier semaphores. Data moves between devices by JAX's collectives and lax.ppermute only.
A program may use at most 64 MiB of HBM per device.

```python
import math
import jax
import jax.numpy as jnp
import numpy as np
from jax import lax

D = 4096
FF = 1536
EXPERTS = 64
TOPK = 8
TOK_ROW = 32
CAP = 8
TOKENS = 1024
SLOTS = 256
FF_BLOCK = 48
N_EXPERT = 32
N_FSDP = 32


def shard_levels(stream_key, extent, cuts, smallest, top_value):
    loudness = 1.0
    for axis_at, shards_of in cuts:
        draws = jax.random.uniform(jax.random.fold_in(jax.random.fold_in(stream_key, 6), axis_at), (shards_of,), jnp.float32, smallest / len(cuts), top_value / len(cuts))
        loudness = loudness * jnp.repeat(jnp.exp(draws), extent[axis_at] // shards_of).reshape((-1,) + (1,) * (len(extent) - 1 - axis_at))
    return loudness


def deal_out(own_key, own, number, rows, count, top, limit, lean):
    sequence = jax.random.permutation(own_key, count)
    packed, common = portions_of(count, rows * top, limit, lean, True), portions_of(count, rows * top, limit, lean, False)
    places = jnp.arange(count)

    def named(tallies, turn):
        used = int((tallies > 0).sum())
        fixed = max(1, used // 4)
        moved = fixed + (places - fixed + turn * (used - fixed)) % max(1, count - fixed)
        return jnp.zeros((count,), jnp.int32).at[sequence[jnp.where(places < fixed, places, moved)]].set(jnp.asarray(tallies, jnp.int32))

    tallies = jnp.where(number % 4 == 0, named(packed, number // 4), named(common, number - number // 4 - 1))
    mixed = jax.random.permutation(jax.random.fold_in(own, 3), count)
    donor, sink = mixed[0:count // 2 * 2:2], mixed[1:count // 2 * 2:2]
    slack = jnp.minimum(tallies[donor] - 1, limit - tallies[sink]) // 2
    slack = jnp.where((donor == sequence[0]) | (sink == sequence[0]) | (tallies[sink] == 0), 0, jnp.maximum(slack, 0))
    moved = jax.random.randint(jax.random.fold_in(own, 4), (count // 2,), 0, 1 << 20) % (slack + 1)
    tallies = tallies.at[donor].add(-moved).at[sink].add(moved)
    items = jnp.searchsorted(jnp.cumsum(tallies), jnp.arange(rows * top), side="right").astype(jnp.int32)
    listing = items.reshape(top, rows).T
    listing = listing[jax.random.permutation(jax.random.fold_in(own, 1), rows)]
    turn = jax.random.randint(jax.random.fold_in(own, 2), (rows, 1), 0, top)
    return jnp.take_along_axis(listing, (jnp.arange(top)[None, :] + turn) % top, axis=1)


def portions_of(count, total, limit, skew, full):
    loads = [(1 << 20) // math.isqrt(rank ** skew) + 1 for rank in range(1, count + 1)]
    largest = limit if full else min(limit, max(-(-total // count), total * loads[0] // sum(loads)))
    least = 1 if total - largest >= count - 1 else 0
    counts, rest = [largest] + [least] * (count - 1), total - largest - least * (count - 1)
    while rest > 0:
        movable = [i for i in range(1, count) if counts[i] < largest] or [i for i in range(1, count) if counts[i] < limit]
        mass, budget = sum([loads[i] for i in movable]), rest
        for i in movable:
            more = min(limit - counts[i], max(1, budget * loads[i] // mass), rest)
            counts[i] = counts[i] + more
            rest = rest - more
    return np.array(counts)


def gaussian(rng, dims, scale, reach, cuts=(), kind=jnp.bfloat16):
    loudness = shard_levels(rng, dims, cuts, -0.22, 0.18) if cuts else 1.0
    result = jax.random.normal(rng, dims, jnp.float32) * scale * loudness
    return jnp.minimum(jnp.maximum(result, -reach), reach).astype(kind)


def setup_inputs(seed: int = 0) -> dict:
    seeds = jax.random.split(jax.random.key(seed), 5)
    tokens = gaussian(seeds[0], (TOKENS, D), 1.0, 6.0, ((0, 32), (1, 32)))
    expert_ids_keys = jax.random.split(jax.random.fold_in(seeds[1], 1), TOKENS // TOK_ROW)
    expert_ids_turns = jax.random.permutation(jax.random.fold_in(seeds[1], 3), TOKENS // TOK_ROW)
    expert_ids = jax.vmap(lambda own, number: deal_out(jax.random.fold_in(seeds[1], 2), own, number, TOK_ROW, EXPERTS, TOPK, CAP, 2))(expert_ids_keys, expert_ids_turns).reshape((TOKENS, TOPK))
    gate_up = gaussian(seeds[2], (EXPERTS, 2, FF, D), D ** -0.5, 0.09375, ((0, 32), (2, 32)))
    hidden_grad = gaussian(seeds[3], (EXPERTS, FF, SLOTS), 0.25, 1.5, ((0, 32), (1, 32)))
    return {"tokens": tokens, "expert_ids": expert_ids, "gate_up": gate_up, "hidden_grad": hidden_grad}


def slot_layout(expert_ids):
    blocks = expert_ids.astype(jnp.int32).reshape(N_EXPERT, TOK_ROW, TOPK)
    expert_iota = jnp.arange(EXPERTS, dtype=jnp.int32)
    chosen = jnp.sum((blocks[:, :, :, None] == expert_iota).astype(jnp.int32), axis=2)
    before = jnp.cumsum(chosen, axis=1) - chosen
    slot_iota = jnp.arange(CAP, dtype=jnp.int32)
    placed = (chosen[:, :, :, None] == 1) & (before[:, :, :, None] == slot_iota)
    return placed.astype(jnp.float32)


def expert_pass(items):
    routed_x, weights, grad_hidden = items
    gate_value = jnp.dot(weights[0], routed_x.T, preferred_element_type=jnp.float32)
    up_value = jnp.dot(weights[1], routed_x.T, preferred_element_type=jnp.float32)
    sigmoid_gate = 1.0 / (1.0 + jnp.exp(-gate_value))
    active = gate_value * sigmoid_gate
    hidden = (active * up_value).astype(jnp.bfloat16)
    grad_value = grad_hidden.astype(jnp.float32)
    gate_grad = (grad_value * up_value * sigmoid_gate * (1.0 + gate_value * (1.0 - sigmoid_gate))).astype(jnp.bfloat16)
    up_grad = (grad_value * active).astype(jnp.bfloat16)
    weight_grad = jnp.stack([
        jnp.dot(gate_grad, routed_x, preferred_element_type=jnp.float32),
        jnp.dot(up_grad, routed_x, preferred_element_type=jnp.float32),
    ]).astype(jnp.bfloat16)
    block_grads = jnp.stack([gate_grad, up_grad]).astype(jnp.float32).reshape(2, N_FSDP, FF_BLOCK, SLOTS)
    block_weights = weights.astype(jnp.float32).reshape(2, N_FSDP, FF_BLOCK, D)
    parts = jnp.einsum("wqis,wqid->qsd", block_grads, block_weights, precision=lax.Precision.HIGHEST)
    parts = lax.optimization_barrier(parts.astype(jnp.bfloat16)).astype(jnp.float32)
    return hidden, weight_grad, jnp.sum(parts, axis=0)


def reference(tokens, expert_ids, gate_up, hidden_grad):
    placed = slot_layout(expert_ids)
    blocks = tokens.astype(jnp.float32).reshape(N_EXPERT, TOK_ROW, D)
    routed = jnp.einsum("btxc,btd->xbcd", placed, blocks, precision=lax.Precision.HIGHEST)
    routed = routed.reshape(EXPERTS, SLOTS, D).astype(jnp.bfloat16)
    hidden, weight_grad, slot_total = lax.map(expert_pass, (routed, gate_up, hidden_grad))
    slot_total = slot_total.reshape(EXPERTS, N_EXPERT, CAP, D)
    token_grad = jnp.einsum("btxc,xbcd->btd", placed, slot_total, precision=lax.Precision.HIGHEST)
    return hidden, weight_grad, token_grad.reshape(TOKENS, D).astype(jnp.bfloat16)
```

```python
import functools

import jax
import jax.numpy as jnp
from jax import lax
from jax.experimental import pallas as pl
from jax.experimental.pallas import tpu as pltpu
from jax.sharding import Mesh, PartitionSpec as P

LANES = 128
BF16 = jnp.bfloat16
F32 = jnp.float32
VMEM = pltpu.VMEM
XN = 4


def dot(a, b, ca, cb):
    return lax.dot_general(a, b, (((ca,), (cb,)), ((), ())), preferred_element_type=F32)


def call(body, outs, flops, nbytes, *args):
    specs = [
        pl.BlockSpec(memory_space=pltpu.SMEM if a.dtype == jnp.int32 else VMEM) for a in args
    ]
    return pl.pallas_call(
        body,
        out_shape=[jax.ShapeDtypeStruct(s, d) for s, d in outs],
        in_specs=specs,
        out_specs=[pl.BlockSpec(memory_space=VMEM) for _ in outs],
        cost_estimate=pl.CostEstimate(flops=flops, bytes_accessed=nbytes, transcendentals=0),
    )(*args)


def lane_block(i):
    return pl.ds(pl.multiple_of(i * LANES, LANES), LANES)


def shift(v, axis, k):
    n = lax.axis_size(axis)
    return lax.ppermute(v, axis, [(i, (i + k) % n) for i in range(n)])


def split_body(yn, at, w, *outs):
    for j, out in enumerate(outs):
        xj = lax.rem(at[0] + j, XN)
        for y in range(yn):
            out[:, y * LANES : (y + 1) * LANES] = w[:, lane_block(y * XN + xj)]


def join_body(yn, at, *refs):
    out = refs[-1]
    for j, part in enumerate(refs[:-1]):
        xj = lax.rem(at[0] + j, XN)
        for y in range(yn):
            out[:, lane_block(y * XN + xj)] = part[:, y * LANES : (y + 1) * LANES]


def forward_body(yn, at, *refs):
    chunks, last, weights = refs[: yn - 1], refs[yn - 1 : yn + 1], refs[yn + 1 : yn + 1 + XN]
    rows, sums = refs[yn + 1 + XN], refs[yn + 2 + XN :]
    experts = rows.shape[0]
    half = yn // 2
    units = weights[0].shape[0] // experts
    for e in range(experts):
        for k in range(yn):
            where = lane_block(lax.rem(at[1] + k, yn))
            if k == half:
                rows[e, :, where] = last[e][0]
            else:
                rows[e, :, where] = chunks[k if k < half else k - 1][e]
        left = jnp.concatenate([w[e * units : (e + 1) * units] for w in weights], axis=0)
        total = dot(left, rows[e], 1, 1)
        for j, out in enumerate(sums):
            out[e] = total[j * units : (j + 1) * units].astype(out.dtype)


def gate_body(s0, s1, s2, s3, hg, hidden, grads):
    half = hg.shape[1]
    for e in range(hg.shape[0]):
        total = s0[e] + s1[e].astype(F32) + s2[e].astype(F32) + s3[e].astype(F32)
        gate, up = total[:half], total[half:]
        sig = 1.0 / (1.0 + jnp.exp(-gate))
        active = gate * sig
        g = hg[e].astype(F32)
        hidden[e] = (active * up).astype(BF16)
        grads[e, :half] = (g * up * sig * (1.0 + gate * (1.0 - sig))).astype(BF16)
        grads[e, half:] = (g * active).astype(BF16)


def backward_body(*refs):
    grads, weights, rows = refs[:XN], refs[XN : 2 * XN], refs[2 * XN]
    part, wgrads = refs[2 * XN + 1], refs[2 * XN + 2 :]
    experts, units = grads[0].shape[0], grads[0].shape[1]
    for e in range(experts):
        g = jnp.concatenate([v[e] for v in grads], axis=0)
        left = jnp.concatenate([w[e * units : (e + 1) * units] for w in weights], axis=0)
        sent = dot(g, left, 0, 0).astype(BF16)
        for y in range(part.shape[0]):
            part[y, e] = sent[:, y * LANES : (y + 1) * LANES]
        back = dot(g, rows[e], 1, 0).astype(BF16)
        for j, out in enumerate(wgrads):
            out[e * units : (e + 1) * units] = back[j * units : (j + 1) * units]


def dispatch_table(expert_ids, groups, local_experts, capacity):
    every = groups * local_experts
    expert_iota = jnp.arange(every, dtype=jnp.int32)
    chosen = jnp.sum((expert_ids[:, :, None] == expert_iota).astype(jnp.int32), axis=1)
    before = jnp.cumsum(chosen, axis=0) - chosen
    slot_iota = jnp.arange(capacity, dtype=jnp.int32)
    placed = (chosen.T[:, None, :] == 1) & (before.T[:, None, :] == slot_iota[None, :, None])
    return placed.reshape(groups, local_experts, capacity, expert_ids.shape[0])


def exchange_x(v1, v2, v3):
    from_left = shift(v1, "x", 1)
    from_right = shift(v3, "x", -1)
    return from_right, shift(v2, "x", 2), from_left


def local(tokens, expert_ids, gate_up, hidden_grad):
    groups = lax.axis_size("expert")
    yn = lax.axis_size("y")
    experts, _, units, width = gate_up.shape
    rows_w = experts * 2 * units
    slots = hidden_grad.shape[2]
    capacity = slots // groups
    quarter = width // XN
    at = jnp.stack([lax.axis_index("x"), lax.axis_index("y")]).astype(jnp.int32)

    flat = gate_up.reshape(rows_w, width)
    w0, o1, o2, o3 = call(
        functools.partial(split_body, yn),
        [((rows_w, quarter), BF16)] * XN,
        0, 4 * rows_w * width, at, flat,
    )
    w1, w2, w3 = exchange_x(o1, o2, o3)

    selector = dispatch_table(expert_ids, groups, experts, capacity).astype(BF16)
    outgoing = jnp.einsum("gjct,td->gjcd", selector, tokens, preferred_element_type=F32).astype(BF16)
    arrived = lax.all_to_all(outgoing, "expert", split_axis=0, concat_axis=0, tiled=True)
    own = jnp.transpose(arrived, (1, 0, 2, 3)).reshape(experts, slots, LANES)

    half = yn // 2
    near = {0: own}
    up, down = own, own
    for k in range(1, half):
        up, down = shift(up, "y", 1), shift(down, "y", -1)
        near[yn - k], near[k] = up, down
    last = [shift(up[:1], "y", 1), shift(down[1:], "y", -1)]
    chunks = [near[k] for k in range(yn) if k != half]

    flops = 2 * 4 * rows_w * quarter * slots
    rows, p0, p1, p2, p3 = call(
        functools.partial(forward_body, yn),
        [((experts, slots, quarter), BF16), ((experts, 2 * units, slots), F32)]
        + [((experts, 2 * units, slots), BF16)] * 3,
        flops, 4 << 20, at, *chunks, *last, w0, w1, w2, w3,
    )
    q1, q2, q3 = exchange_x(p1, p2, p3)
    hidden, g0 = call(
        gate_body,
        [((experts, units, slots), BF16), ((experts, 2 * units, slots), BF16)],
        20 * rows_w * slots, 1 << 20, p0, q1, q2, q3, hidden_grad,
    )
    g1, g2, g3 = exchange_x(g0, g0, g0)
    part, b0, b1, b2, b3 = call(
        backward_body,
        [((yn, experts, slots, LANES), BF16)] + [((rows_w, quarter), BF16)] * XN,
        2 * flops, 6 << 20, g0, g1, g2, g3, w0, w1, w2, w3, rows,
    )
    c1, c2, c3 = exchange_x(b1, b2, b3)
    parts = lax.all_to_all(part, "y", split_axis=0, concat_axis=0, tiled=True)
    summed = jnp.sum(parts.astype(F32), axis=0).astype(BF16)
    summed = jnp.transpose(summed.reshape(experts, groups, capacity, LANES), (1, 0, 2, 3))
    returned = lax.all_to_all(summed, "expert", split_axis=0, concat_axis=0, tiled=True)
    token_grad = jnp.einsum(
        "gjct,gjcd->td", selector, returned, preferred_element_type=F32
    ).astype(BF16)
    (weight_grad,) = call(
        functools.partial(join_body, yn),
        [((rows_w, width), BF16)],
        0, 4 * rows_w * width, at, b0, c1, c2, c3,
    )
    return hidden, weight_grad.reshape(gate_up.shape), token_grad


def solution(mesh):
    n_expert, n_fsdp = mesh.devices.shape
    grid = Mesh(mesh.devices.reshape(n_expert, n_fsdp // XN, XN), ("expert", "y", "x"))
    fsdp = ("y", "x")
    placed = (
        P("expert", fsdp),
        P("expert", None),
        P("expert", None, fsdp, None),
        P("expert", fsdp, None),
    )
    return jax.shard_map(
        local,
        mesh=grid,
        in_specs=placed,
        out_specs=(P("expert", fsdp, None), P("expert", None, fsdp, None), P("expert", fsdp)),
        check_vma=False,
    )
```

```python
import jax
import jax.numpy as jnp
from jax import lax
from jax.experimental import pallas as pl
from jax.experimental.pallas import tpu as pltpu
from jax.sharding import Mesh, PartitionSpec as P


LANES = 128
BF16 = jnp.bfloat16
F32 = jnp.float32
XN = 4


def dot(a, b, ca, cb):
    return lax.dot_general(a, b, (((ca,), (cb,)), ((), ())), preferred_element_type=F32)


def call(body, outs, flops, nbytes, *args):
    return pl.pallas_call(
        body,
        out_shape=[jax.ShapeDtypeStruct(s, d) for s, d in outs],
        in_specs=[
            pl.BlockSpec(memory_space=pltpu.SMEM if a.dtype == jnp.int32 else pltpu.VMEM)
            for a in args
        ],
        out_specs=[pl.BlockSpec(memory_space=pltpu.VMEM) for _ in outs],
        cost_estimate=pl.CostEstimate(flops=flops, bytes_accessed=nbytes, transcendentals=0),
        compiler_params=pltpu.CompilerParams(vmem_limit_bytes=20 << 20),
    )(*args)


def lanes(i):
    return slice(i * LANES, (i + 1) * LANES)


def swap(v, axis):
    return lax.all_to_all(v, axis, split_axis=0, concat_axis=0, tiled=True)


def lane_block(i):
    return pl.ds(pl.multiple_of(i * LANES, LANES), LANES)


def shift(v, axis, k):
    n = lax.axis_size(axis)
    return lax.ppermute(v, axis, [(i, (i + k) % n) for i in range(n)])


def exchange_x(v1, v2, v3):
    from_left = shift(v1, "x", 1)
    from_right = shift(v3, "x", -1)
    return from_right, shift(v2, "x", 2), from_left


def split_body(at, w, *outs):
    for j, out in enumerate(outs):
        xj = lax.rem(at[0] + j, XN)
        for y in range(w.shape[1] // (XN * LANES)):
            out[:, lanes(y)] = w[:, lane_block(y * XN + xj)]


def join_body(at, *refs):
    out = refs[-1]
    for j, part in enumerate(refs[:-1]):
        xj = lax.rem(at[0] + j, XN)
        for y in range(part.shape[1] // LANES):
            out[:, lane_block(y * XN + xj)] = part[:, lanes(y)]


def forward_body(at, chunks, *refs):
    weights, rows, sums = refs[:XN], refs[XN], refs[XN + 1]
    yn, experts = chunks.shape[:2]
    units = weights[0].shape[0] // experts
    for e in range(experts):
        for y in range(yn):
            rows[e, :, lanes(y)] = chunks[y, e]
        left = jnp.concatenate([w[e * units : (e + 1) * units] for w in weights], axis=0)
        total = dot(left, rows[e], 1, 1).astype(BF16)
        for j in range(XN):
            sums[lax.rem(at[0] + j, XN), e] = total[j * units : (j + 1) * units]


def gate_body(sums, hg, hidden, grads):
    half = hg.shape[1]
    for e in range(hg.shape[0]):
        total = sums[0, e].astype(F32)
        for x in range(1, XN):
            total = total + sums[x, e].astype(F32)
        gate, up = total[:half], total[half:]
        sig = 1.0 / (1.0 + jnp.exp(-gate))
        active = gate * sig
        g = hg[e].astype(F32)
        hidden[e] = (active * up).astype(BF16)
        gate_grad = (g * up * sig * (1.0 + gate * (1.0 - sig))).astype(BF16)
        up_grad = (g * active).astype(BF16)
        for x in range(grads.shape[0]):
            grads[x, e, :half] = gate_grad
            grads[x, e, half:] = up_grad


def backward_body(at, grads, *refs):
    weights, rows, part, wgrads = refs[:XN], refs[XN], refs[XN + 1], refs[XN + 2 :]
    experts, units = grads.shape[1], grads.shape[2]
    for e in range(experts):
        g = jnp.concatenate([grads[lax.rem(at[0] + j, XN), e] for j in range(XN)], axis=0)
        left = jnp.concatenate([w[e * units : (e + 1) * units] for w in weights], axis=0)
        back = dot(g, rows[e], 1, 0).astype(BF16)
        for j, out in enumerate(wgrads):
            out[e * units : (e + 1) * units] = back[j * units : (j + 1) * units]
        sent = dot(g, left, 0, 0).astype(BF16)
        for y in range(part.shape[0]):
            part[y, e] = sent[:, lanes(y)]


def dispatch_table(expert_ids, groups, local_experts, capacity):
    every = groups * local_experts
    expert_iota = jnp.arange(every, dtype=jnp.int32)
    chosen = jnp.sum((expert_ids[:, :, None] == expert_iota).astype(jnp.int32), axis=1)
    before = jnp.cumsum(chosen, axis=0) - chosen
    slot_iota = jnp.arange(capacity, dtype=jnp.int32)
    placed = (chosen.T[:, None, :] == 1) & (before.T[:, None, :] == slot_iota[None, :, None])
    return placed.reshape(groups, local_experts, capacity, expert_ids.shape[0])


def body(tokens, expert_ids, gate_up, hidden_grad):
    groups = lax.axis_size("expert")
    yn = lax.axis_size("y")
    experts, _, units, width = gate_up.shape
    rows_w = experts * 2 * units
    slots = hidden_grad.shape[2]
    capacity = slots // groups
    quarter = width // XN

    at = lax.axis_index("x").astype(jnp.int32)[None]

    flat = gate_up.reshape(rows_w, width)
    w0, o1, o2, o3 = call(
        split_body, [((rows_w, quarter), BF16)] * XN, 0, 4 * rows_w * width, at, flat
    )
    weights = (w0,) + exchange_x(o1, o2, o3)

    selector = dispatch_table(expert_ids, groups, experts, capacity).astype(BF16)
    outgoing = jnp.einsum("gjct,td->gjcd", selector, tokens, preferred_element_type=F32).astype(BF16)
    arrived = swap(outgoing, "expert")
    own = jnp.transpose(arrived, (1, 0, 2, 3)).reshape(experts, slots, LANES)
    chunks = swap(jnp.broadcast_to(own[None], (yn,) + own.shape), "y")

    flops = 2 * 4 * rows_w * quarter * slots
    rows, sums = call(
        forward_body,
        [((experts, slots, quarter), BF16), ((XN, experts, 2 * units, slots), BF16)],
        flops, 4 << 20, at, chunks, *weights,
    )
    sums = swap(sums, "x")
    hidden, grads = call(
        gate_body,
        [((experts, units, slots), BF16), ((XN, experts, 2 * units, slots), BF16)],
        20 * rows_w * slots, 1 << 20, sums, hidden_grad,
    )
    grads = swap(grads, "x")
    part, b0, b1, b2, b3 = call(
        backward_body,
        [((yn, experts, slots, LANES), BF16)] + [((rows_w, quarter), BF16)] * XN,
        2 * flops, 6 << 20, at, grads, *weights, rows,
    )
    parts = swap(part, "y")
    back = (b0,) + exchange_x(b1, b2, b3)
    summed = jnp.sum(parts.astype(F32), axis=0).astype(BF16)
    summed = jnp.transpose(summed.reshape(experts, groups, capacity, LANES), (1, 0, 2, 3))
    returned = swap(summed, "expert")
    token_grad = jnp.einsum(
        "gjct,gjcd->td", selector, returned, preferred_element_type=F32
    ).astype(BF16)
    (weight_grad,) = call(join_body, [((rows_w, width), BF16)], 0, 4 * rows_w * width, at, *back)
    return hidden, weight_grad.reshape(gate_up.shape), token_grad


def solution(mesh):
    n_expert, n_fsdp = mesh.devices.shape
    grid = Mesh(mesh.devices.reshape(n_expert, n_fsdp // XN, XN), ("expert", "y", "x"))
    fsdp = ("y", "x")
    placed = (
        P("expert", fsdp),
        P("expert", None),
        P("expert", None, fsdp, None),
        P("expert", fsdp, None),
    )
    return jax.shard_map(
        body,
        mesh=grid,
        in_specs=placed,
        out_specs=(P("expert", fsdp, None), P("expert", None, fsdp, None), P("expert", fsdp)),
        check_vma=False,
    )
```

```python
import functools

import jax
import jax.numpy as jnp
from jax import lax
from jax.experimental import pallas as pl
from jax.experimental.pallas import tpu as pltpu
from jax.sharding import Mesh, PartitionSpec as P


LANES = 128
BF16 = jnp.bfloat16
F32 = jnp.float32
XN = 4


def dot(a, b, ca, cb):
    return lax.dot_general(a, b, (((ca,), (cb,)), ((), ())), preferred_element_type=F32)


def call(body, outs, flops, nbytes, *args, fetch=False):
    return pl.pallas_call(
        body,
        out_shape=[jax.ShapeDtypeStruct(s, d) for s, d in outs],
        in_specs=[
            pl.BlockSpec()
            if fetch
            else pl.BlockSpec(memory_space=pltpu.SMEM if a.ndim == 1 else pltpu.VMEM)
            for a in args
        ],
        out_specs=[pl.BlockSpec(memory_space=pltpu.VMEM) for _ in outs],
        cost_estimate=pl.CostEstimate(flops=flops, bytes_accessed=nbytes, transcendentals=0),
        compiler_params=pltpu.CompilerParams(vmem_limit_bytes=(60 if fetch else 20) << 20),
    )(*args)


def lanes(i):
    return slice(i * LANES, (i + 1) * LANES)


def swap(v, axis):
    return lax.all_to_all(v, axis, split_axis=0, concat_axis=0, tiled=True)


def lane_block(i):
    return pl.ds(pl.multiple_of(i * LANES, LANES), LANES)


def shift(v, axis, k):
    n = lax.axis_size(axis)
    return lax.ppermute(v, axis, [(i, (i + k) % n) for i in range(n)])


def gather_y(own):
    n = lax.axis_size("y")
    half = n // 2
    near = {0: own}
    up, down = own, own
    middle = own.shape[0] // 2
    for k in range(1, half):
        if k == half - 1:
            last = [(up[:middle], 2), (down[middle:], -2)]
        up, down = shift(up, "y", 1), shift(down, "y", -1)
        near[n - k], near[k] = up, down
    last = [shift(v, "y", k) for v, k in last]
    return [near[k] for k in range(n) if k != half] + last


def exchange_x(v1, v2, v3):
    from_left = shift(v1, "x", 1)
    from_right = shift(v3, "x", -1)
    return from_right, shift(v2, "x", 2), from_left


def split_body(at, w, *outs):
    for j, out in enumerate(outs):
        xj = lax.rem(at[0] + j, XN)
        for y in range(w.shape[1] // (XN * LANES)):
            out[:, lanes(y)] = w[:, lane_block(y * XN + xj)]


def join_body(at, *refs):
    out = refs[-1]
    for j, part in enumerate(refs[:-1]):
        xj = lax.rem(at[0] + j, XN)
        for y in range(part.shape[1] // LANES):
            out[:, lane_block(y * XN + xj)] = part[:, lanes(y)]


def forward_body(yn, at, at_y, *refs):
    chunks, last, refs = refs[: yn - 1], refs[yn - 1 : yn + 1], refs[yn + 1 :]
    weights, rows, sums = refs[:XN], refs[XN], refs[XN + 1]
    experts, half = rows.shape[0], yn // 2
    units = weights[0].shape[0] // experts
    for e in range(experts):
        for k in range(yn):
            where = lane_block(lax.rem(at_y[0] + k, yn))
            if k == half:
                rows[e, :, where] = last[2 * e // experts][e % (experts // 2)]
            else:
                rows[e, :, where] = chunks[k if k < half else k - 1][e]
        left = jnp.concatenate([w[e * units : (e + 1) * units] for w in weights], axis=0)
        total = dot(left, rows[e], 1, 1).astype(BF16)
        for j in range(XN):
            sums[lax.rem(at[0] + j, XN), e] = total[j * units : (j + 1) * units]


def gate_body(sums, hg, hidden, grads):
    half = hg.shape[1]
    for e in range(hg.shape[0]):
        total = sums[0, e].astype(F32)
        for x in range(1, XN):
            total = total + sums[x, e].astype(F32)
        gate, up = total[:half], total[half:]
        sig = 1.0 / (1.0 + jnp.exp(-gate))
        active = gate * sig
        g = hg[e].astype(F32)
        hidden[e] = (active * up).astype(BF16)
        gate_grad = (g * up * sig * (1.0 + gate * (1.0 - sig))).astype(BF16)
        up_grad = (g * active).astype(BF16)
        for x in range(grads.shape[0]):
            grads[x, e, :half] = gate_grad
            grads[x, e, half:] = up_grad


def backward_body(at, grads, *refs):
    weights, rows, part, wgrads = refs[:XN], refs[XN], refs[XN + 1], refs[XN + 2 :]
    experts, units = grads.shape[1], grads.shape[2]
    for e in range(experts):
        g = jnp.concatenate([grads[lax.rem(at[0] + j, XN), e] for j in range(XN)], axis=0)
        left = jnp.concatenate([w[e * units : (e + 1) * units] for w in weights], axis=0)
        back = dot(g, rows[e], 1, 0).astype(BF16)
        for j, out in enumerate(wgrads):
            out[e * units : (e + 1) * units] = back[j * units : (j + 1) * units]
        sent = dot(g, left, 0, 0).astype(BF16)
        for y in range(part.shape[0]):
            part[y, e] = sent[:, lanes(y)]


def pick_body(capacity, ids, tokens, rows, pick):
    count, block = ids.shape
    every = rows.shape[0]
    experts = every // capacity
    named = lax.broadcasted_iota(jnp.int32, (experts, block), 0)
    chosen = jnp.zeros((experts, block), F32)
    for k in range(count):
        chosen = chosen + jnp.where(ids[k : k + 1, :] == named, 1.0, 0.0)
    earlier = lax.broadcasted_iota(jnp.int32, (block, block), 0) < lax.broadcasted_iota(
        jnp.int32, (block, block), 1
    )
    chosen = chosen.astype(BF16)
    before = dot(chosen, jnp.where(earlier, 1.0, 0.0).astype(BF16), 1, 0).astype(BF16)
    slot = lax.broadcasted_iota(jnp.int32, (every, experts), 0)
    expert = lax.broadcasted_iota(jnp.int32, (every, experts), 1)
    spread = jnp.where(lax.div(slot, capacity) == expert, 1.0, 0.0).astype(BF16)
    place = lax.rem(lax.broadcasted_iota(jnp.int32, (every, block), 0), capacity).astype(F32)
    here = (dot(spread, chosen, 1, 0) > 0.5) & (dot(spread, before, 1, 0) == place)
    matrix = jnp.where(here, 1.0, 0.0).astype(BF16)
    pick[...] = matrix
    rows[...] = dot(matrix, tokens[...], 1, 0).astype(BF16)


def fold_body(pick, rows, out):
    out[...] = dot(pick[...], rows[...], 0, 0).astype(BF16)


def sum_body(parts, out):
    capacity = out.shape[2]
    for e in range(out.shape[1]):
        total = parts[0, e].astype(F32)
        for y in range(1, parts.shape[0]):
            total = total + parts[y, e].astype(F32)
        for g in range(out.shape[0]):
            out[g, e] = total[g * capacity : (g + 1) * capacity].astype(BF16)


def body(tokens, expert_ids, gate_up, hidden_grad):
    groups = lax.axis_size("expert")
    yn = lax.axis_size("y")
    experts, _, units, width = gate_up.shape
    rows_w = experts * 2 * units
    slots = hidden_grad.shape[2]
    capacity = slots // groups
    quarter = width // XN

    at = lax.axis_index("x").astype(jnp.int32)[None]
    at_y = lax.axis_index("y").astype(jnp.int32)[None]

    flat = gate_up.reshape(rows_w, width)
    w0, o1, o2, o3 = call(
        split_body, [((rows_w, quarter), BF16)] * XN, 0, 4 * rows_w * width, at, flat
    )
    weights = (w0,) + exchange_x(o1, o2, o3)

    ids = jnp.transpose(expert_ids)
    every = experts * slots
    outgoing, pick = call(
        functools.partial(pick_body, capacity),
        [((every, LANES), BF16), ((every, ids.shape[1]), BF16)],
        1 << 22, 1 << 18, ids, tokens, fetch=True,
    )
    arrived = swap(outgoing.reshape(groups, experts, capacity, LANES), "expert")
    own = jnp.transpose(arrived, (1, 0, 2, 3)).reshape(experts, slots, LANES)
    chunks = gather_y(own)

    flops = 2 * 4 * rows_w * quarter * slots
    rows, sums = call(
        functools.partial(forward_body, yn),
        [((experts, slots, quarter), BF16), ((XN, experts, 2 * units, slots), BF16)],
        flops, 4 << 20, at, at_y, *chunks, *weights,
    )
    sums = swap(sums, "x")
    hidden, grads = call(
        gate_body,
        [((experts, units, slots), BF16), ((XN, experts, 2 * units, slots), BF16)],
        20 * rows_w * slots, 1 << 20, sums, hidden_grad,
    )
    grads = swap(grads, "x")
    part, b0, b1, b2, b3 = call(
        backward_body,
        [((yn, experts, slots, LANES), BF16)] + [((rows_w, quarter), BF16)] * XN,
        2 * flops, 6 << 20, at, grads, *weights, rows,
    )
    parts = swap(part, "y")
    back = (b0,) + exchange_x(b1, b2, b3)
    (summed,) = call(
        sum_body, [((groups, experts, capacity, LANES), BF16)], 1 << 20, 2 << 20, parts
    )
    returned = swap(summed, "expert")
    (token_grad,) = call(
        fold_body, [(tokens.shape, BF16)], 1 << 22, 1 << 18, pick, returned.reshape(every, LANES)
    )
    (weight_grad,) = call(join_body, [((rows_w, width), BF16)], 0, 4 * rows_w * width, at, *back)
    return hidden, weight_grad.reshape(gate_up.shape), token_grad


def solution(mesh):
    n_expert, n_fsdp = mesh.devices.shape
    grid = Mesh(mesh.devices.reshape(n_expert, n_fsdp // XN, XN), ("expert", "y", "x"))
    fsdp = ("y", "x")
    placed = (
        P("expert", fsdp),
        P("expert", None),
        P("expert", None, fsdp, None),
        P("expert", fsdp, None),
    )
    return jax.shard_map(
        body,
        mesh=grid,
        in_specs=placed,
        out_specs=(P("expert", fsdp, None), P("expert", None, fsdp, None), P("expert", fsdp)),
        check_vma=False,
    )
```

```python
import functools

import jax
import jax.numpy as jnp
from jax import lax
from jax.experimental import pallas as pl
from jax.experimental.pallas import tpu as pltpu
from jax.sharding import Mesh, PartitionSpec as P


LANES = 128
BF16 = jnp.bfloat16
F32 = jnp.float32
XN = 4


def dot(a, b, ca, cb):
    return lax.dot_general(a, b, (((ca,), (cb,)), ((), ())), preferred_element_type=F32)


def call(body, outs, flops, nbytes, *args, fetch=False):
    return pl.pallas_call(
        body,
        out_shape=[jax.ShapeDtypeStruct(s, d) for s, d in outs],
        in_specs=[
            pl.BlockSpec()
            if fetch
            else pl.BlockSpec(memory_space=pltpu.SMEM if a.ndim == 1 else pltpu.VMEM)
            for a in args
        ],
        out_specs=[pl.BlockSpec(memory_space=pltpu.VMEM) for _ in outs],
        cost_estimate=pl.CostEstimate(flops=flops, bytes_accessed=nbytes, transcendentals=0),
        compiler_params=pltpu.CompilerParams(vmem_limit_bytes=(60 if fetch else 20) << 20),
    )(*args)


def lanes(i):
    return slice(i * LANES, (i + 1) * LANES)


def swap(v, axis):
    return lax.all_to_all(v, axis, split_axis=0, concat_axis=0, tiled=True)


def lane_block(i):
    return pl.ds(pl.multiple_of(i * LANES, LANES), LANES)


def shift(v, axis, k):
    n = lax.axis_size(axis)
    return lax.ppermute(v, axis, [(i, (i + k) % n) for i in range(n)])


def gather_y(own):
    n = lax.axis_size("y")
    half = n // 2
    up, down = shift(own, "y", 1), shift(own, "y", -1)
    got = {0: own, half: shift(own, "y", half), n - 1: up, 1: down}
    for k in range(2, half):
        up, down = shift(up, "y", 1), shift(down, "y", -1)
        got[n - k], got[k] = up, down
    return [got[k] for k in range(n)]


def exchange_x(v1, v2, v3):
    from_left = shift(v1, "x", 1)
    from_right = shift(v3, "x", -1)
    return from_right, shift(v2, "x", 2), from_left


def split_body(at, w, *outs):
    for j, out in enumerate(outs):
        xj = lax.rem(at[0] + j, XN)
        for y in range(w.shape[1] // (XN * LANES)):
            out[:, lanes(y)] = w[:, lane_block(y * XN + xj)]


def join_body(at, *refs):
    out = refs[-1]
    for j, part in enumerate(refs[:-1]):
        xj = lax.rem(at[0] + j, XN)
        for y in range(part.shape[1] // LANES):
            out[:, lane_block(y * XN + xj)] = part[:, lanes(y)]


def forward_body(yn, at, at_y, *refs):
    chunks, refs = refs[:yn], refs[yn:]
    weights, rows, sums = refs[:XN], refs[XN], refs[XN + 1]
    experts = rows.shape[0]
    units = weights[0].shape[0] // experts
    for e in range(experts):
        for k in range(yn):
            where = lane_block(lax.rem(at_y[0] + k, yn))
            rows[e, :, where] = chunks[k][e]
        left = jnp.concatenate([w[e * units : (e + 1) * units] for w in weights], axis=0)
        total = dot(left, rows[e], 1, 1).astype(BF16)
        for j in range(XN):
            sums[lax.rem(at[0] + j, XN), e] = total[j * units : (j + 1) * units]


def gate_body(sums, hg, hidden, grads):
    half = hg.shape[1]
    for e in range(hg.shape[0]):
        total = sums[0, e].astype(F32)
        for x in range(1, XN):
            total = total + sums[x, e].astype(F32)
        gate, up = total[:half], total[half:]
        sig = 1.0 / (1.0 + jnp.exp(-gate))
        active = gate * sig
        g = hg[e].astype(F32)
        hidden[e] = (active * up).astype(BF16)
        gate_grad = (g * up * sig * (1.0 + gate * (1.0 - sig))).astype(BF16)
        up_grad = (g * active).astype(BF16)
        for x in range(grads.shape[0]):
            grads[x, e, :half] = gate_grad
            grads[x, e, half:] = up_grad


def backward_body(at, grads, *refs):
    weights, rows, part, wgrads = refs[:XN], refs[XN], refs[XN + 1], refs[XN + 2 :]
    experts, units = grads.shape[1], grads.shape[2]
    for e in range(experts):
        g = jnp.concatenate([grads[lax.rem(at[0] + j, XN), e] for j in range(XN)], axis=0)
        left = jnp.concatenate([w[e * units : (e + 1) * units] for w in weights], axis=0)
        back = dot(g, rows[e], 1, 0).astype(BF16)
        for j, out in enumerate(wgrads):
            out[e * units : (e + 1) * units] = back[j * units : (j + 1) * units]
        sent = dot(g, left, 0, 0).astype(BF16)
        for y in range(part.shape[0]):
            part[y, e] = sent[:, lanes(y)]


def pick_body(capacity, ids, tokens, rows, pick):
    count, block = ids.shape
    every = rows.shape[0]
    experts = every // capacity
    named = lax.broadcasted_iota(jnp.int32, (experts, block), 0)
    chosen = jnp.zeros((experts, block), F32)
    for k in range(count):
        chosen = chosen + jnp.where(ids[k : k + 1, :] == named, 1.0, 0.0)
    earlier = lax.broadcasted_iota(jnp.int32, (block, block), 0) < lax.broadcasted_iota(
        jnp.int32, (block, block), 1
    )
    chosen = chosen.astype(BF16)
    before = dot(chosen, jnp.where(earlier, 1.0, 0.0).astype(BF16), 1, 0).astype(BF16)
    slot = lax.broadcasted_iota(jnp.int32, (every, experts), 0)
    expert = lax.broadcasted_iota(jnp.int32, (every, experts), 1)
    spread = jnp.where(lax.div(slot, capacity) == expert, 1.0, 0.0).astype(BF16)
    place = lax.rem(lax.broadcasted_iota(jnp.int32, (every, block), 0), capacity).astype(F32)
    here = (dot(spread, chosen, 1, 0) > 0.5) & (dot(spread, before, 1, 0) == place)
    matrix = jnp.where(here, 1.0, 0.0).astype(BF16)
    pick[...] = matrix
    rows[...] = dot(matrix, tokens[...], 1, 0).astype(BF16)


def fold_body(pick, rows, out):
    out[...] = dot(pick[...], rows[...], 0, 0).astype(BF16)


def sum_body(parts, out):
    capacity = out.shape[2]
    for e in range(out.shape[1]):
        total = parts[0, e].astype(F32)
        for y in range(1, parts.shape[0]):
            total = total + parts[y, e].astype(F32)
        for g in range(out.shape[0]):
            out[g, e] = total[g * capacity : (g + 1) * capacity].astype(BF16)


def body(tokens, expert_ids, gate_up, hidden_grad):
    groups = lax.axis_size("expert")
    yn = lax.axis_size("y")
    experts, _, units, width = gate_up.shape
    rows_w = experts * 2 * units
    slots = hidden_grad.shape[2]
    capacity = slots // groups
    quarter = width // XN

    at = lax.axis_index("x").astype(jnp.int32)[None]
    at_y = lax.axis_index("y").astype(jnp.int32)[None]

    flat = gate_up.reshape(rows_w, width)
    w0, o1, o2, o3 = call(
        split_body, [((rows_w, quarter), BF16)] * XN, 0, 4 * rows_w * width, at, flat
    )
    weights = (w0,) + exchange_x(o1, o2, o3)

    ids = jnp.transpose(expert_ids)
    every = experts * slots
    outgoing, pick = call(
        functools.partial(pick_body, capacity),
        [((every, LANES), BF16), ((every, ids.shape[1]), BF16)],
        1 << 22, 1 << 18, ids, tokens, fetch=True,
    )
    arrived = swap(outgoing.reshape(groups, experts, capacity, LANES), "expert")
    own = jnp.transpose(arrived, (1, 0, 2, 3)).reshape(experts, slots, LANES)
    chunks = gather_y(own)

    flops = 2 * 4 * rows_w * quarter * slots
    rows, sums = call(
        functools.partial(forward_body, yn),
        [((experts, slots, quarter), BF16), ((XN, experts, 2 * units, slots), BF16)],
        flops, 4 << 20, at, at_y, *chunks, *weights,
    )
    sums = swap(sums, "x")
    hidden, grads = call(
        gate_body,
        [((experts, units, slots), BF16), ((XN, experts, 2 * units, slots), BF16)],
        20 * rows_w * slots, 1 << 20, sums, hidden_grad,
    )
    grads = swap(grads, "x")
    part, b0, b1, b2, b3 = call(
        backward_body,
        [((yn, experts, slots, LANES), BF16)] + [((rows_w, quarter), BF16)] * XN,
        2 * flops, 6 << 20, at, grads, *weights, rows,
    )
    parts = swap(part, "y")
    back = (b0,) + exchange_x(b1, b2, b3)
    (summed,) = call(
        sum_body, [((groups, experts, capacity, LANES), BF16)], 1 << 20, 2 << 20, parts
    )
    returned = swap(summed, "expert")
    (token_grad,) = call(
        fold_body, [(tokens.shape, BF16)], 1 << 22, 1 << 18, pick, returned.reshape(every, LANES)
    )
    (weight_grad,) = call(join_body, [((rows_w, width), BF16)], 0, 4 * rows_w * width, at, *back)
    return hidden, weight_grad.reshape(gate_up.shape), token_grad


def solution(mesh):
    n_expert, n_fsdp = mesh.devices.shape
    grid = Mesh(mesh.devices.reshape(n_expert, n_fsdp // XN, XN), ("expert", "y", "x"))
    fsdp = ("y", "x")
    placed = (
        P("expert", fsdp),
        P("expert", None),
        P("expert", None, fsdp, None),
        P("expert", fsdp, None),
    )
    return jax.shard_map(
        body,
        mesh=grid,
        in_specs=placed,
        out_specs=(P("expert", fsdp, None), P("expert", None, fsdp, None), P("expert", fsdp)),
        check_vma=False,
    )
```
